1024 devices in a mesh: dp: 32 (over x_lo, z), tensor: 32 (over x_hi, y, core).
Axes of the slice: x: 4 (x_hi: 2, x_lo: 2; x = x_hi * 2 + x_lo), y: 8, z: 16, core: 2. Of those that a mesh axis runs over, the one named last changes fastest.
Arguments:
- queries: bfloat16 [32, 133, 4096], P('dp', None, 'tensor'), may hold values from -50 to 50
- keys: bfloat16 [32, 1024, 4096], P('dp', None, 'tensor'), may hold values from -4 to 4
- values: bfloat16 [32, 1024, 4096], P('dp', None, 'tensor'), may hold values from -6 to 6
- conv_kernel: float32 [32, 6, 11], P('tensor'), may hold values from -0.9 to 1.9
- span_start: int32 [32], P('dp'), may hold values from 0 to 896, as said below
- out_grad: bfloat16 [32, 128, 4096], P('dp', None, 'tensor'), may hold values from -6 to 6
- proj_weight: float32 [4096, 4096], P('tensor', 'dp'), may hold values from -0.09375 to 0.09375
- moment_one: float32 [4096, 4096], P('tensor', 'dp'), may hold values from -12 to 12
- moment_two: float32 [4096, 4096], P('tensor', 'dp'), may hold values from 1 to 100
Outputs:
- query_grad: bfloat16 [32, 133, 4096], P('dp', None, 'tensor')
- key_grad: bfloat16 [32, 1024, 4096], P('dp', None, 'tensor')
- value_grad: bfloat16 [32, 1024, 4096], P('dp', None, 'tensor')
- kernel_grad: float32 [32, 6, 11], P('tensor')
- proj_new: float32 [4096, 4096], P('tensor', 'dp')
- moment_one_new: float32 [4096, 4096], P('tensor', 'dp')
- moment_two_new: float32 [4096, 4096], P('tensor', 'dp')
The draws below stay inside these ranges and needn't reach their ends.
Inputs may be any that keep to these rules, and one draw needn't show every extreme that they name: `span_start`: each sequence's first block row; one sequence starts at 0 and one at 896.
All inputs are finite; a program needn't handle non-finite values.
Results may differ from the reference program's by a relative error of at most 0.0029.
The reference program's roundings to bfloat16 on the way count: a program that leaves them out, or rounds other values in their place, can miss the bound.
Values may be sent and summed in bfloat16 or wider, within the bound.
A program may use at most 32 MiB of HBM per device.

```python
import math
import jax
import jax.numpy as jnp
from jax import lax

HEADS = 32
D = 4096
CQ = 6
CK = 11
SPAN = 128
KEYS = 1024
QROWS = 133
GROUPS = 32


def draw_keys(key, part):
    return jnp.clip(jax.random.normal(jax.random.fold_in(key, 24), (GROUPS, KEYS, D), jnp.float32), -4.0, 4.0).astype(jnp.bfloat16)


def draw_queries(key, part):
    return jnp.clip(jax.random.normal(jax.random.fold_in(key, 32), (GROUPS, QROWS, D), jnp.float32), -4.0, 4.0).astype(jnp.bfloat16)


def draw_conv_kernel(key, part):
    taps = jnp.clip(0.3 * jax.random.normal(jax.random.fold_in(key, 42), (HEADS, CQ, CK), jnp.float32), -0.9, 0.9)
    centre = (jnp.arange(CQ)[:, None] == 0) & (jnp.arange(CK)[None, :] == (CK - 1) // 2)
    return taps + centre.astype(jnp.float32)[None, :, :]


def draw_span_start(key, part):
    picks = jax.random.randint(jax.random.fold_in(key, 51), (GROUPS,), 0, KEYS - SPAN + 1)
    order = jax.random.permutation(jax.random.fold_in(key, 52), GROUPS)
    picks = picks.at[order[0]].set(KEYS - SPAN)
    picks = picks.at[order[1]].set(0)
    return picks.astype(jnp.int32)


def block_scale(stream_key, shape, pieces, low, top_value):
    factor_of, own = 1.0, jax.random.fold_in(stream_key, 6)
    for axis_at, blocks in pieces:
        heights = jnp.exp(jax.random.uniform(jax.random.fold_in(own, axis_at), (blocks,), jnp.float32, low / len(pieces), top_value / len(pieces)))
        factor_of = factor_of * jnp.repeat(heights, shape[axis_at] // blocks).reshape([-1 if axis == axis_at else 1 for axis in range(len(shape))])
    return factor_of


def gaussian(rng, dims, deviation, limit, split=(), held_as=jnp.bfloat16):
    factor_of = block_scale(rng, dims, split, -0.22, 0.18) if split else 1.0
    drawn = jax.random.normal(rng, dims, jnp.float32) * deviation * factor_of
    return jnp.minimum(jnp.maximum(drawn, -limit), limit).astype(held_as)


def setup_inputs(seed: int = 0) -> dict:
    arg_keys = jax.random.split(jax.random.key(seed), 10)
    return {
        "queries": draw_queries(jax.random.fold_in(arg_keys[9], 71), 0),
        "keys": draw_keys(jax.random.fold_in(arg_keys[9], 71), 0),
        "values": gaussian(arg_keys[2], (GROUPS, KEYS, D), 1.0, 6.0, ((0, 32), (2, 32))),
        "conv_kernel": draw_conv_kernel(jax.random.fold_in(arg_keys[9], 71), 0),
        "span_start": draw_span_start(jax.random.fold_in(arg_keys[9], 71), 0),
        "out_grad": gaussian(arg_keys[5], (GROUPS, SPAN, D), 1.0, 6.0, ((0, 32), (2, 32))),
        "proj_weight": gaussian(arg_keys[6], (D, D), D ** -0.5, 0.09375, ((0, 32), (1, 32)), jnp.float32),
        "moment_one": gaussian(arg_keys[7], (D, D), 3.0, 12.0, ((0, 32), (1, 32)), jnp.float32),
        "moment_two": jnp.clip(jnp.exp(math.log(100.0) - 4.6051702 * jax.random.uniform(arg_keys[8], (D, D), jnp.float32) ** block_scale(arg_keys[8], (D, D), ((0, 32), (1, 32)), -0.2, 0.2)), 1.0, 100.0),
    }


beta_one = 0.9
beta_two = 0.95
learn_rate = 0.01
decay_rate = 0.1
adam_eps = 1e-08
bias_one = 1.0 - 0.9 ** 10
bias_two = 1.0 - 0.95 ** 10

def head_backward(query_rows, key_rows, value_rows, kernel, proj_rows, first_pos, upstream):
    conv_rows = kernel.shape[0]
    conv_cols = kernel.shape[1]
    half_width = (conv_cols - 1) // 2
    span_len = upstream.shape[0]
    key_count = key_rows.shape[0]
    query_count = query_rows.shape[0]
    score_scale = 1.0 / query_rows.shape[1] ** 0.5
    key_pos = jnp.arange(key_count, dtype=jnp.int32)
    row_pos = first_pos - (conv_rows - 1) + jnp.arange(query_count, dtype=jnp.int32)
    visible = key_pos[None, :] <= row_pos[:, None]
    raw_scores = jnp.dot(query_rows, key_rows.T, preferred_element_type=jnp.float32) * score_scale
    masked = jnp.where(visible, raw_scores, 0.0)
    padded = jnp.pad(masked, ((0, 0), (half_width, half_width)))
    mixed_scores = jnp.zeros((span_len, key_count), jnp.float32)
    for tap_row in range(conv_rows):
        for tap_col in range(conv_cols):
            row_first = conv_rows - 1 - tap_row
            mixed_scores = mixed_scores + kernel[tap_row, tap_col] * padded[row_first:row_first + span_len, tap_col:tap_col + key_count]
    live_mask = visible[conv_rows - 1:]
    row_top = lax.optimization_barrier(jnp.max(jnp.where(live_mask, mixed_scores, -jnp.inf), axis=1, keepdims=True))
    exp_terms = jnp.where(live_mask, jnp.exp(mixed_scores - row_top), 0.0)
    weights_soft = exp_terms / lax.optimization_barrier(jnp.sum(exp_terms, axis=1, keepdims=True))
    weights_bf = weights_soft.astype(jnp.bfloat16)
    attended = jnp.dot(weights_bf, value_rows, preferred_element_type=jnp.float32).astype(jnp.bfloat16)
    grad_out = jnp.dot(upstream, proj_rows.T, preferred_element_type=jnp.float32).astype(jnp.bfloat16)
    grad_values = jnp.dot(weights_bf.T, grad_out, preferred_element_type=jnp.float32).astype(jnp.bfloat16)
    grad_weights = jnp.dot(grad_out, value_rows.T, preferred_element_type=jnp.float32)
    row_inner = lax.optimization_barrier(jnp.sum(weights_soft * grad_weights, axis=1, keepdims=True))
    grad_mixed = weights_soft * (grad_weights - row_inner)
    grad_pad = jnp.pad(grad_mixed, ((conv_rows - 1, conv_rows - 1), (half_width, half_width)))
    grad_masked = jnp.zeros((query_count, key_count), jnp.float32)
    kernel_terms = []
    for tap_row in range(conv_rows):
        for tap_col in range(conv_cols):
            col_first = 2 * half_width - tap_col
            grad_masked = grad_masked + kernel[tap_row, tap_col] * grad_pad[tap_row:tap_row + query_count, col_first:col_first + key_count]
            row_first = conv_rows - 1 - tap_row
            kernel_terms.append(jnp.sum(grad_mixed * padded[row_first:row_first + span_len, tap_col:tap_col + key_count]))
    kernel_grad = jnp.stack(kernel_terms).reshape(conv_rows, conv_cols)
    grad_scores = jnp.where(visible, grad_masked, 0.0).astype(jnp.bfloat16)
    grad_query = (score_scale * jnp.dot(grad_scores, key_rows, preferred_element_type=jnp.float32)).astype(jnp.bfloat16)
    grad_keys = (score_scale * jnp.dot(grad_scores.T, query_rows, preferred_element_type=jnp.float32)).astype(jnp.bfloat16)
    proj_term = jnp.dot(attended.T, upstream, preferred_element_type=jnp.float32)
    return (grad_query, grad_keys, grad_values, kernel_grad, proj_term)

def split_heads(array_in, head_count):
    return array_in.reshape(array_in.shape[0], head_count, -1).transpose(1, 0, 2)

def join_heads(array_in):
    return array_in.transpose(1, 0, 2).reshape(array_in.shape[1], -1)

def reference(queries, keys, values, conv_kernel, span_start, out_grad, proj_weight, moment_one, moment_two):
    head_count = conv_kernel.shape[0]
    width = proj_weight.shape[0]
    head_dim = width // head_count
    group_count = queries.shape[0]
    span_len = out_grad.shape[1]
    proj_bf = proj_weight.astype(jnp.bfloat16).reshape(head_count, head_dim, width)

    def group_step(state_pair, group_items):
        proj_total, kernel_total = state_pair
        query_g, key_g, value_g, first_pos, upstream = group_items

        def per_head(head_items):
            return head_backward(head_items[0], head_items[1], head_items[2], head_items[3], head_items[4], first_pos, upstream)
        results = lax.map(per_head, (split_heads(query_g, head_count), split_heads(key_g, head_count), split_heads(value_g, head_count), conv_kernel, proj_bf))
        grad_query, grad_keys, grad_values, kernel_part, proj_part = results
        proj_total = proj_total + proj_part.reshape(width, width)
        kernel_total = kernel_total + kernel_part
        return ((proj_total, kernel_total), (join_heads(grad_query), join_heads(grad_keys), join_heads(grad_values)))
    start_state = (jnp.zeros((width, width), jnp.float32), jnp.zeros(conv_kernel.shape, jnp.float32))
    finals, grads = lax.scan(group_step, start_state, (queries, keys, values, span_start, out_grad))
    proj_sum, kernel_sum = finals
    grad_proj = proj_sum / float(group_count)
    kernel_grad = kernel_sum / float(group_count * span_len)
    query_grad, key_grad, value_grad = grads
    moment_one_new = beta_one * moment_one + (1.0 - beta_one) * grad_proj
    moment_two_new = beta_two * moment_two + (1.0 - beta_two) * grad_proj * grad_proj
    first_hat = moment_one_new / bias_one
    second_hat = moment_two_new / bias_two
    proj_new = proj_weight - learn_rate * (first_hat / (jnp.sqrt(second_hat) + adam_eps) + decay_rate * proj_weight)
    return (query_grad, key_grad, value_grad, kernel_grad, proj_new, moment_one_new, moment_two_new)
```

```python
import functools
import math

import jax
import jax.numpy as jnp
from jax import lax
from jax.experimental import pallas as pl
from jax.experimental.pallas import tpu as pltpu
from jax.sharding import PartitionSpec as P

beta_one = 0.9
beta_two = 0.95
learn_rate = 0.01
decay_rate = 0.1
adam_eps = 1e-08
bias_one = 1.0 - 0.9**10
bias_two = 1.0 - 0.95**10

MESH = pl.DeviceIdType.MESH
F32 = jnp.float32
BF16 = jnp.bfloat16
NX, NZ, NY = 2, 16, 8
STEP_Z, STEP_Y = 2, 1
CR, CC = 6, 11
HALF = 5
TILE = 32


def dot_cols(left, right):
    return lax.dot_general(
        left, right, (((1,), (1,)), ((), ())), preferred_element_type=F32
    )


def dot_rows(left, right):
    return lax.dot_general(
        left, right, (((0,), (0,)), ((), ())), preferred_element_type=F32
    )


def dot_mid(left, right):
    return lax.dot_general(
        left, right, (((1,), (0,)), ((), ())), preferred_element_type=F32
    )


def kernel(
    q_ref, k_ref, v_ref, tap_ref, start_ref, og_ref, w_ref, m1_ref, m2_ref,
    dq_ref, dk_ref, dv_ref, kg_ref, wn_ref, m1n_ref, m2n_ref,
    w_all, o_all, u_all, t_all, xp, prob, prob_bf, dcp, ds, qp, taps, acc, kg_all, dpp,
    do_bf,
    w_send, w_recv, o_send, o_recv, u_send, u_recv, t_send, t_recv, p_send, kg_send, kg_recv,
):
    d = lax.axis_index("dp")
    t = lax.axis_index("tensor")
    dp_count = NX * NZ
    z, xl = lax.rem(d, NZ), d // NZ
    core, yy = lax.rem(t, 2), lax.rem(t // 2, NY)
    xh = t // (2 * NY)
    scale = 1.0 / math.sqrt(k_ref.shape[2])
    blocks = k_ref.shape[1] // 128

    def dp_at(x, zz):
        return x * NZ + lax.rem(zz + 2 * NZ, NZ)

    def tn_at(x, y, c):
        return (x * NY + lax.rem(y + 2 * NY, NY)) * 2 + c

    pending = []

    def push(buf, index, sends, slot, recvs, target):
        copy = pltpu.make_async_remote_copy(
            src_ref=buf.at[index], dst_ref=buf.at[index],
            send_sem=sends.at[slot], recv_sem=recvs.at[index],
            device_id=target, device_id_type=MESH,
        )
        copy.start()
        pending.append(copy)

    def arrive(buf, index, recvs):
        pltpu.make_async_remote_copy(
            src_ref=buf.at[index], dst_ref=buf.at[index],
            send_sem=p_send.at[0], recv_sem=recvs.at[index],
            device_id=(d, t), device_id_type=MESH,
        ).wait_recv()

    up, down = NZ // 2, NZ - 1 - NZ // 2

    class GatherDp:
        def __init__(self, buf, sends, recvs):
            self.buf, self.sends, self.recvs, self.slot = buf, sends, recvs, 0

        def push(self, index, target):
            push(self.buf, index, self.sends, self.slot, self.recvs, target)
            self.slot += 1

        def ring(self, at):
            for q in range(1, STEP_Z + 1):
                if at + q <= up:
                    self.push(dp_at(xl, z - at), (dp_at(xl, z + q), t))
                if at + q <= down:
                    self.push(dp_at(xl, z + at), (dp_at(xl, z - q), t))

        def cross(self, offset):
            self.push(dp_at(xl, z + offset), (dp_at(1 - xl, z), t))

        def begin(self):
            self.ring(0)
            self.cross(0)

        def stage(self, number):
            first = number * STEP_Z
            near = []
            for q in range(STEP_Z, 0, -1):
                for sign, limit in ((-1, up), (1, down)):
                    if first + q <= limit:
                        arrive(self.buf, dp_at(xl, z + sign * (first + q)), self.recvs)
                        near.append(sign * (first + q))
                if q == STEP_Z:
                    self.ring(first + q)
            for offset in near:
                self.cross(offset)

        stages = -(-up // STEP_Z)

        def finish(self):
            for other in range(NZ):
                arrive(self.buf, dp_at(1 - xl, z + other), self.recvs)

    y_up, y_down = NY // 2, NY - 1 - NY // 2

    class GatherTn:
        def __init__(self, buf, sends, recvs):
            self.buf, self.sends, self.recvs, self.slot = buf, sends, recvs, 0

        def push(self, index, target):
            push(self.buf, index, self.sends, self.slot, self.recvs, target)
            self.slot += 1

        def ring(self, x, at):
            for q in range(1, STEP_Y + 1):
                if at + q <= y_up:
                    self.push(tn_at(x, yy - at, core), (d, tn_at(xh, yy + q, core)))
                if at + q <= y_down:
                    self.push(tn_at(x, yy + at, core), (d, tn_at(xh, yy - q, core)))

        def mate(self, x, offset):
            self.push(tn_at(x, yy + offset, core), (d, tn_at(xh, yy, 1 - core)))

        def begin(self):
            self.push(t, (d, tn_at(1 - xh, yy, core)))
            self.ring(xh, 0)
            self.mate(xh, 0)

        def crossed(self):
            arrive(self.buf, tn_at(1 - xh, yy, core), self.recvs)
            self.ring(1 - xh, 0)
            self.mate(1 - xh, 0)

        def stage(self, number, x):
            first = number * STEP_Y
            near = []
            for q in range(STEP_Y, 0, -1):
                for sign, limit in ((-1, y_up), (1, y_down)):
                    if first + q <= limit:
                        arrive(self.buf, tn_at(x, yy + sign * (first + q), core), self.recvs)
                        near.append(sign * (first + q))
                if q == STEP_Y:
                    self.ring(x, first + q)
            for offset in near:
                self.mate(x, offset)

        stages = -(-y_up // STEP_Y)

        def both(self, number):
            self.stage(number, xh)
            self.stage(number, 1 - xh)

        def finish(self):
            for x in range(2):
                for other in range(NY):
                    arrive(self.buf, tn_at(x, yy + other, 1 - core), self.recvs)

    gw = GatherDp(w_all, w_send, w_recv)
    go = GatherDp(o_all, o_send, o_recv)
    gu = GatherTn(u_all, u_send, u_recv)
    gt = GatherTn(t_all, t_send, t_recv)

    w_all[d] = w_ref[...].astype(BF16)
    u_all[t] = og_ref[0]

    targets = [(dp_at(1 - xl, z), t), (d, tn_at(1 - xh, yy, core)), (d, tn_at(xh, yy, 1 - core))]
    for q in range(1, STEP_Z + 1):
        targets += [(dp_at(xl, z + q), t), (dp_at(xl, z - q), t)]
    for q in range(1, STEP_Y + 1):
        targets += [(d, tn_at(xh, yy + q, core)), (d, tn_at(xh, yy - q, core))]
    barrier = pltpu.get_barrier_semaphore()
    for target in targets:
        pl.semaphore_signal(barrier, inc=1, device_id=target, device_id_type=MESH)
    pl.semaphore_signal(barrier, inc=1, device_id=(t, d), device_id_type=MESH)

    qp[pl.ds(128, 16), :] = jnp.zeros((16, 128), BF16)
    qp[pl.ds(0, q_ref.shape[1]), :] = q_ref[0]
    for edge in (0, blocks + 1):
        xp[edge] = jnp.zeros((xp.shape[1], 128), F32)
        dcp[edge] = jnp.zeros((dcp.shape[1], 128), F32)
    for inner in range(1, blocks + 1):
        dcp[inner, pl.ds(0, 8), :] = jnp.zeros((8, 128), F32)
        dcp[inner, pl.ds(136, 16), :] = jnp.zeros((16, 128), F32)
    for a in range(CR):
        for b in range(CC):
            taps[a * CC + b] = jnp.full((8, 128), tap_ref[0, a, b], F32)
    acc[...] = jnp.zeros(acc.shape, F32)

    pl.semaphore_wait(barrier, len(targets) + 1)

    gw.begin()
    gu.begin()

    transpose = pltpu.make_async_remote_copy(
        src_ref=u_all.at[t], dst_ref=t_all.at[d],
        send_sem=p_send.at[0], recv_sem=t_recv.at[d],
        device_id=(t, d), device_id_type=MESH,
    )

    @pl.when(d != t)
    def _():
        transpose.start()

    @pl.when(d == t)
    def _():
        t_all[t] = og_ref[0]

    start = start_ref[0]

    def lanes(rows):
        return lax.broadcasted_iota(jnp.int32, (rows, 128), 1)

    def sublanes(rows):
        return lax.broadcasted_iota(jnp.int32, (rows, 128), 0)

    def visible(jb, rows, first):
        return jb * 128 + lanes(rows) <= start + (first + sublanes(rows))

    def shifted(prev, cur, nxt, by):
        if by == 0:
            return cur
        lane = lanes(cur.shape[0])
        if by > 0:
            return pltpu.roll(jnp.where(lane >= by, cur, nxt), 128 - by, 1)
        return pltpu.roll(jnp.where(lane < 128 + by, cur, prev), -by, 1)

    def score_block(jb, carry):
        keys = k_ref[0, pl.ds(pl.multiple_of(jb * 128, 128), 128), :]
        raw = dot_cols(qp[...], keys) * scale
        xp[jb + 1] = jnp.where(visible(jb, xp.shape[1], -HALF), raw, 0.0)
        return carry

    lax.fori_loop(0, blocks, score_block, 0)

    def row_sums(src, jb, first, rows, flip):
        prev = src[jb, pl.ds(first, rows), :]
        cur = src[jb + 1, pl.ds(first, rows), :]
        nxt = src[jb + 2, pl.ds(first, rows), :]
        sums = [None] * CR
        for b in range(CC):
            moved = shifted(prev, cur, nxt, (HALF - b) if flip else (b - HALF))
            moved = moved.reshape(rows // 8, 8, 128)
            for a in range(CR):
                term = taps[a * CC + b][None] * moved
                sums[a] = term if b == 0 else sums[a] + term
        return [s.reshape(rows, 128) for s in sums]

    def forward_tile(tile):
        first = tile * TILE
        rows = TILE + 8

        def mix(jb, top):
            sums = row_sums(xp, jb, first, rows, False)
            total = sums[CR - 1]
            for a in range(CR - 1):
                total = total + pltpu.roll(sums[a], rows - (HALF - a), 0)
            total = jnp.where(visible(jb, TILE, first), total[:TILE], -jnp.inf)
            prob[jb, pl.ds(first, TILE), :] = total
            return jnp.maximum(top, total)

        top = lax.fori_loop(0, blocks, mix, jnp.full((TILE, 128), -jnp.inf, F32))
        top = jnp.max(top, axis=1, keepdims=True)

        total = jnp.zeros((TILE, 128), F32)
        for jb in range(blocks):
            term = jnp.exp(prob[jb, pl.ds(first, TILE), :] - top)
            prob[jb, pl.ds(first, TILE), :] = term
            total = total + term
        inverse = 1.0 / jnp.sum(total, axis=1, keepdims=True)
        out = jnp.zeros((TILE, 128), F32)
        for jb in range(blocks):
            weight = prob[jb, pl.ds(first, TILE), :] * inverse
            prob[jb, pl.ds(first, TILE), :] = weight
            rounded = weight.astype(BF16)
            prob_bf[jb, pl.ds(first, TILE), :] = rounded
            out = out + dot_mid(rounded, v_ref[0, pl.ds(jb * 128, 128), :])
        o_all[d, pl.ds(first, TILE), :] = out.astype(BF16)

    forward_tile(0)
    gu.crossed()
    gw.stage(0)
    gu.stage(0, xh)
    forward_tile(1)
    gu.stage(0, 1 - xh)
    gu.stage(1, xh)

    @pl.when(d != t)
    def _():
        pltpu.make_async_remote_copy(
            src_ref=u_all.at[t], dst_ref=t_all.at[t],
            send_sem=p_send.at[0], recv_sem=t_recv.at[t],
            device_id=(t, d), device_id_type=MESH,
        ).wait_recv()

    gt.begin()
    forward_tile(2)
    gw.stage(1)
    gu.stage(1, 1 - xh)
    gu.stage(2, xh)
    forward_tile(3)
    gw.stage(2)
    go.begin()
    gu.stage(2, 1 - xh)
    gu.stage(3, xh)
    gt.crossed()
    gt.stage(0, xh)
    gu.stage(3, 1 - xh)
    gt.stage(0, 1 - xh)
    gw.stage(3)
    go.stage(0)
    gt.both(1)
    gu.finish()
    gw.finish()

    grad_out = jnp.zeros((128, 128), F32)
    for c in range(dp_count // 2):
        left = jnp.concatenate([u_all[2 * c], u_all[2 * c + 1]], axis=1)
        right = jnp.concatenate([w_all[2 * c], w_all[2 * c + 1]], axis=1)
        grad_out = grad_out + dot_cols(left, right)
    do_bf[...] = grad_out.astype(BF16)

    inner = jnp.zeros((128, 128), F32)
    for jb in range(blocks):
        part = dot_cols(do_bf[...], v_ref[0, pl.ds(jb * 128, 128), :])
        dpp[jb] = part
        inner = inner + prob[jb] * part
    inner = jnp.sum(inner, axis=1, keepdims=True)
    for jb in range(blocks):
        dcp[jb + 1, pl.ds(8, 128), :] = prob[jb] * (dpp[jb] - inner)

    def tap_grads(tile):
        first = tile * TILE
        rows = TILE + 8

        def body(jb, carry):
            wide = xp[jb + 1, pl.ds(first, rows), :]
            scores = []
            for a in range(CR):
                turned = wide if a == CR - 1 else pltpu.roll(wide, rows - (HALF - a), 0)
                scores.append(turned[:TILE].reshape(TILE // 8, 8, 128))
            prev = dcp[jb, pl.ds(8 + first, TILE), :]
            cur = dcp[jb + 1, pl.ds(8 + first, TILE), :]
            nxt = dcp[jb + 2, pl.ds(8 + first, TILE), :]
            for b in range(CC):
                moved = shifted(prev, cur, nxt, HALF - b).reshape(TILE // 8, 8, 128)
                for a in range(CR):
                    acc[a * 16 + b] += jnp.sum(scores[a] * moved, axis=0)
            return carry

        lax.fori_loop(0, blocks, body, 0)

    def grad_tile(first, count):
        rows = count + 8

        def body(jb, carry):
            sums = row_sums(dcp, jb, first, rows, True)
            total = None
            for a in range(CR):
                turned = pltpu.roll(sums[a], rows - (3 + a), 0)[:count]
                total = turned if total is None else total + turned
            total = jnp.where(visible(jb, count, first - HALF), total, 0.0)
            ds[jb, pl.ds(first, count), :] = total.astype(BF16)
            return carry

        lax.fori_loop(0, blocks, body, 0)

    tap_grads(0)
    tap_grads(1)
    go.stage(1)
    gt.both(2)
    tap_grads(2)
    tap_grads(3)

    folded = jnp.sum(acc[...], axis=1)
    kg_row = lax.dot_general(
        jnp.ones((8, 128), F32), folded, (((1,), (1,)), ((), ())),
        preferred_element_type=F32, precision=lax.Precision.HIGHEST,
    )
    kg_all[d] = kg_row[0:1]
    go.stage(2)
    gt.both(3)
    for r in range(1, dp_count):
        push(kg_all, d, kg_send, r, kg_recv, (lax.rem(d + r, dp_count), t))

    grad_tile(0, TILE)
    grad_tile(TILE, TILE)
    go.stage(3)
    grad_tile(2 * TILE, TILE)
    grad_tile(3 * TILE, TILE)
    grad_tile(4 * TILE, 16)

    grad_query = jnp.zeros((qp.shape[0], 128), F32)
    for jb in range(blocks):
        span = pl.ds(jb * 128, 128)
        grad_query = grad_query + dot_mid(ds[jb], k_ref[0, span, :])
        dk_ref[0, span, :] = (scale * dot_rows(ds[jb], qp[...])).astype(BF16)
        dv_ref[0, span, :] = dot_rows(prob_bf[jb], do_bf[...]).astype(BF16)
    dq_ref[0] = (scale * grad_query[: q_ref.shape[1]]).astype(BF16)

    gt.finish()
    go.finish()
    total = jnp.zeros((128, 128), F32)
    for g in range(dp_count // 2):
        left = jnp.concatenate([o_all[2 * g], o_all[2 * g + 1]], axis=0)
        right = jnp.concatenate([t_all[2 * g], t_all[2 * g + 1]], axis=0)
        total = total + dot_rows(left, right)
    grad = total * (1.0 / dp_count)
    one = beta_one * m1_ref[...] + (1.0 - beta_one) * grad
    two = beta_two * m2_ref[...] + (1.0 - beta_two) * grad * grad
    m1n_ref[...] = one
    m2n_ref[...] = two
    wn_ref[...] = w_ref[...] - learn_rate * (
        (one / bias_one) / (jnp.sqrt(two / bias_two) + adam_eps) + decay_rate * w_ref[...]
    )

    for r in range(1, dp_count):
        arrive(kg_all, lax.rem(d + r, dp_count), kg_recv)
    kg_sum = kg_all[0]
    for r in range(1, dp_count):
        kg_sum = kg_sum + kg_all[r]
    kg_sum = kg_sum * (1.0 / (dp_count * 128))
    for a in range(CR):
        row = kg_sum if a == 0 else pltpu.roll(kg_sum, 128 - 16 * a, 1)
        kg_ref[0, pl.ds(a, 1), :] = row[:, :CC]

    for copy in pending:
        copy.wait_send()

    @pl.when(d != t)
    def _():
        transpose.wait_send()


def shards(*args):
    queries, keys = args[0], args[1]
    proj = args[6]
    vmem = pl.BlockSpec(memory_space=pltpu.VMEM)
    smem = pl.BlockSpec(memory_space=pltpu.SMEM)
    dma = pltpu.SemaphoreType.DMA
    outs = (
        jax.ShapeDtypeStruct(queries.shape, BF16),
        jax.ShapeDtypeStruct(keys.shape, BF16),
        jax.ShapeDtypeStruct(keys.shape, BF16),
        jax.ShapeDtypeStruct(args[3].shape, F32),
        jax.ShapeDtypeStruct(proj.shape, F32),
        jax.ShapeDtypeStruct(proj.shape, F32),
        jax.ShapeDtypeStruct(proj.shape, F32),
    )
    gathered = pltpu.VMEM((32, 128, 128), BF16)
    blocks = keys.shape[1] // 128
    return pl.pallas_call(
        kernel,
        out_shape=outs,
        in_specs=[vmem, vmem, vmem, smem, smem, vmem, vmem, vmem, vmem],
        out_specs=[vmem] * 7,
        scratch_shapes=[
            gathered, gathered, gathered, gathered,
            pltpu.VMEM((blocks + 2, 144, 128), F32),
            pltpu.VMEM((blocks, 128, 128), F32),
            pltpu.VMEM((blocks, 128, 128), BF16),
            pltpu.VMEM((blocks + 2, 152, 128), F32),
            pltpu.VMEM((blocks, 144, 128), BF16),
            pltpu.VMEM((144, 128), BF16),
            pltpu.VMEM((CR * CC, 8, 128), F32),
            pltpu.VMEM((128, 8, 128), F32),
            pltpu.VMEM((32, 1, 128), F32),
            pltpu.VMEM((blocks, 128, 128), F32),
            pltpu.VMEM((128, 128), BF16),
            dma((32,)), dma((32,)), dma((32,)), dma((32,)),
            dma((32,)), dma((32,)), dma((32,)), dma((32,)),
            dma((1,)), dma((32,)), dma((32,)),
        ],
        compiler_params=pltpu.CompilerParams(collective_id=0, has_side_effects=True),
    )(*args)


def solution(mesh):
    heads = P("dp", None, "tensor")
    taps = P("tensor", None, None)
    grid = P("tensor", "dp")
    return jax.shard_map(
        shards,
        mesh=mesh,
        in_specs=(heads, heads, heads, taps, P("dp"), heads, grid, grid, grid),
        out_specs=(heads, heads, heads, taps, grid, grid, grid),
        check_vma=False,
    )
```

```python
import functools
import math

import jax
import jax.numpy as jnp
from jax import lax
from jax.experimental import pallas as pl
from jax.experimental.pallas import tpu as pltpu
from jax.sharding import PartitionSpec as P

beta_one = 0.9
beta_two = 0.95
learn_rate = 0.01
decay_rate = 0.1
adam_eps = 1e-08
bias_one = 1.0 - 0.9**10
bias_two = 1.0 - 0.95**10

MESH = pl.DeviceIdType.MESH
F32 = jnp.float32
BF16 = jnp.bfloat16
NX, NZ, NY = 2, 16, 8
STEP_Z, STEP_Y = 2, 2
CR, CC = 6, 11
HALF = 5
TILE = 32
WIDE = 64


def dot_cols(left, right):
    return lax.dot_general(
        left, right, (((1,), (1,)), ((), ())), preferred_element_type=F32
    )


def dot_rows(left, right):
    return lax.dot_general(
        left, right, (((0,), (0,)), ((), ())), preferred_element_type=F32
    )


def dot_mid(left, right):
    return lax.dot_general(
        left, right, (((1,), (0,)), ((), ())), preferred_element_type=F32
    )


def kernel(
    q_hbm, k_hbm, v_hbm, tap_ref, start_ref, og_hbm, w_hbm, m1_hbm, m2_hbm,
    dq_ref, dk_ref, dv_ref, kg_ref, wn_ref, m1n_ref, m2n_ref,
    w_all, o_all, u_all, t_all, xp, prob, prob_bf, dcp, ds, qp, taps, acc, kg_all, dpp,
    do_bf, q_ref, k_ref, v_ref, w_ref, m1_ref, m2_ref, o_own, load_sem,
    w_send, w_recv, o_send, o_recv, u_send, u_recv, t_send, t_recv, p_send, kg_sem,
):
    d = lax.axis_index("dp")
    t = lax.axis_index("tensor")
    dp_count = NX * NZ
    z, xl = lax.rem(d, NZ), d // NZ
    core, yy = lax.rem(t, 2), lax.rem(t // 2, NY)
    xh = t // (2 * NY)
    scale = 1.0 / math.sqrt(k_ref.shape[2])
    blocks = k_ref.shape[1] // 128

    def dp_at(x, zz):
        return x * NZ + lax.rem(zz + 2 * NZ, NZ)

    def tn_at(x, y, c):
        return (x * NY + lax.rem(y + 2 * NY, NY)) * 2 + c

    def part_of(buf, index, piece, pieces):
        rows = buf.shape[1] // pieces
        return buf.at[index, pl.ds(piece * rows, rows)] if pieces > 1 else buf.at[index]

    def push(ref, send, recv, target):
        pltpu.make_async_remote_copy(
            src_ref=ref, dst_ref=ref, send_sem=send, recv_sem=recv,
            device_id=target, device_id_type=MESH,
        ).start()

    def landed(ref, send, recv):
        return pltpu.make_async_remote_copy(
            src_ref=ref, dst_ref=ref, send_sem=send, recv_sem=recv,
            device_id=(d, t), device_id_type=MESH,
        )

    up, down = NZ // 2, NZ - 1 - NZ // 2

    class GatherDp:
        def __init__(self, buf, sends, recvs, pieces):
            self.buf, self.sends, self.recvs, self.pieces = buf, sends, recvs, pieces

        def ring_sem(self, zz, piece):
            return self.recvs.at[lax.rem(zz + 2 * NZ, NZ) * self.pieces + piece]

        def ring(self, at, piece):
            for q in range(STEP_Z, 0, -1):
                for sign, limit in ((1, up), (-1, down)):
                    if at + q <= limit:
                        ref = part_of(self.buf, dp_at(xl, z - sign * at), piece, self.pieces)
                        push(ref, self.sends.at[0], self.ring_sem(z - sign * at, piece), (dp_at(xl, z + sign * q), t))

        def cross(self, offset, piece):
            ref = part_of(self.buf, dp_at(xl, z + offset), piece, self.pieces)
            push(ref, self.sends.at[0], self.recvs.at[NZ * self.pieces], (dp_at(1 - xl, z), t))

        def begin(self):
            for piece in range(self.pieces):
                self.ring(0, piece)
            for piece in range(self.pieces):
                self.cross(0, piece)

        def stage(self, number):
            first = number * STEP_Z
            for piece in range(self.pieces):
                near = []
                for q in range(STEP_Z, 0, -1):
                    for sign, limit in ((-1, up), (1, down)):
                        if first + q <= limit:
                            offset = sign * (first + q)
                            ref = part_of(self.buf, dp_at(xl, z + offset), piece, self.pieces)
                            landed(ref, self.sends.at[0], self.ring_sem(z + offset, piece)).wait_recv()
                            near.append(offset)
                    if q == STEP_Z:
                        self.ring(first + q, piece)
                for offset in near:
                    self.cross(offset, piece)

        stages = -(-up // STEP_Z)

        def finish(self):
            ref = self.buf.at[pl.ds((1 - xl) * NZ, NZ)]
            landed(ref, self.sends.at[0], self.recvs.at[NZ * self.pieces]).wait_recv()

        def drain(self):
            ref = self.buf.at[pl.ds(0, 2 * NZ - 1)]
            landed(ref, self.sends.at[0], self.recvs.at[0]).wait_send()

    y_up, y_down = NY // 2, NY - 1 - NY // 2

    def slot_of(x, y, c):
        return (c * 2 + x) * NY + lax.rem(y + 2 * NY, NY)

    class GatherTn:
        def __init__(self, buf, sends, recvs):
            self.buf, self.sends, self.recvs = buf, sends, recvs

        def push(self, x, y, sem, target):
            push(self.buf.at[slot_of(x, y, core)], self.sends.at[0], sem, target)

        def ring_sem(self, x, y):
            return self.recvs.at[slot_of(x, y, 0)]

        def ring(self, x, at):
            for q in range(STEP_Y, 0, -1):
                for sign, limit in ((1, y_up), (-1, y_down)):
                    if at + q <= limit:
                        self.push(x, yy - sign * at, self.ring_sem(x, yy - sign * at), (d, tn_at(xh, yy + sign * q, core)))

        def mate(self, x, offset):
            self.push(x, yy + offset, self.recvs.at[2 * NY], (d, tn_at(xh, yy, 1 - core)))

        def begin(self):
            self.push(xh, yy, self.ring_sem(xh, yy), (d, tn_at(1 - xh, yy, core)))
            self.ring(xh, 0)
            self.mate(xh, 0)

        def arrive(self, x, y):
            landed(self.buf.at[slot_of(x, y, core)], self.sends.at[0], self.ring_sem(x, y)).wait_recv()

        def crossed(self):
            self.arrive(1 - xh, yy)
            self.ring(1 - xh, 0)
            self.mate(1 - xh, 0)

        def stage(self, number, x):
            first = number * STEP_Y
            near = []
            for q in range(STEP_Y, 0, -1):
                for sign, limit in ((-1, y_up), (1, y_down)):
                    if first + q <= limit:
                        self.arrive(x, yy + sign * (first + q))
                        near.append(sign * (first + q))
                if q == STEP_Y:
                    self.ring(x, first + q)
            for offset in near:
                self.mate(x, offset)

        stages = -(-y_up // STEP_Y)

        def both(self, number):
            if number < self.stages:
                self.stage(number, xh)
                self.stage(number, 1 - xh)

        def finish(self):
            ref = self.buf.at[pl.ds((1 - core) * 2 * NY, 2 * NY)]
            landed(ref, self.sends.at[0], self.recvs.at[2 * NY]).wait_recv()

        def drain(self):
            ref = self.buf.at[pl.ds(0, 4 * NY - 1)]
            landed(ref, self.sends.at[0], self.recvs.at[0]).wait_send()

    gw = GatherDp(w_all, w_send, w_recv, 2)
    go = GatherDp(o_all, o_send, o_recv, 1)
    gu = GatherTn(u_all, u_send, u_recv)
    gt = GatherTn(t_all, t_send, t_recv)

    mine = slot_of(xh, yy, core)
    theirs = slot_of(d // (2 * NY), lax.rem(d // 2, NY), lax.rem(d, 2))
    loads = []
    for number, (src, dst) in enumerate((
        (w_hbm, w_ref), (og_hbm.at[0], u_all.at[mine]), (q_hbm, q_ref), (k_hbm, k_ref),
        (v_hbm, v_ref), (m1_hbm, m1_ref), (m2_hbm, m2_ref),
    )):
        loads.append(pltpu.make_async_copy(src, dst, load_sem.at[number]))
        loads[-1].start()

    targets = [(dp_at(1 - xl, z), t), (d, tn_at(1 - xh, yy, core)), (d, tn_at(xh, yy, 1 - core))]
    for q in range(1, STEP_Z + 1):
        targets += [(dp_at(xl, z + q), t), (dp_at(xl, z - q), t)]
    for q in range(1, STEP_Y + 1):
        targets += [(d, tn_at(xh, yy + q, core)), (d, tn_at(xh, yy - q, core))]
    barrier = pltpu.get_barrier_semaphore()
    for target in targets:
        pl.semaphore_signal(barrier, inc=1, device_id=target, device_id_type=MESH)
    pl.semaphore_signal(barrier, inc=1, device_id=(t, d), device_id_type=MESH)

    loads[0].wait()
    w_all[d] = w_ref[...].astype(BF16)
    loads[1].wait()
    start = start_ref[0]

    def lanes(rows):
        return lax.broadcasted_iota(jnp.int32, (rows, 128), 1)

    def sublanes(rows):
        return lax.broadcasted_iota(jnp.int32, (rows, 128), 0)

    def visible(jb, rows, first):
        return jb * 128 + lanes(rows) <= start + (first + sublanes(rows))

    def shifted(prev, cur, nxt, by):
        if by == 0:
            return cur
        lane = lanes(cur.shape[0])
        if by > 0:
            return pltpu.roll(jnp.where(lane >= by, cur, nxt), 128 - by, 1)
        return pltpu.roll(jnp.where(lane < 128 + by, cur, prev), -by, 1)

    def score_block(jb, carry):
        keys = k_ref[0, pl.ds(pl.multiple_of(jb * 128, 128), 128), :]
        raw = dot_cols(qp[...], keys) * scale
        xp[jb + 1] = jnp.where(visible(jb, xp.shape[1], -HALF), raw, 0.0)
        return carry

    def row_sums(src, jb, first, rows, flip):
        prev = src[jb, pl.ds(first, rows), :]
        cur = src[jb + 1, pl.ds(first, rows), :]
        nxt = src[jb + 2, pl.ds(first, rows), :]
        groups = (range(0, 3), range(3, CR)) if rows > 40 else (range(CR),)
        sums = [None] * CR
        for group in groups:
            for b in range(CC):
                moved = shifted(prev, cur, nxt, (HALF - b) if flip else (b - HALF))
                moved = moved.reshape(rows // 8, 8, 128)
                for a in group:
                    term = taps[a * CC + b][None] * moved
                    sums[a] = term if b == 0 else sums[a] + term
        return [total.reshape(rows, 128) for total in sums]

    def mix_half(tile, half):
        first = tile * WIDE
        rows = WIDE + 8

        def mix(jb, carry):
            sums = row_sums(xp, jb, first, rows, False)
            total = sums[CR - 1]
            for a in range(CR - 1):
                total = total + pltpu.roll(sums[a], rows - (HALF - a), 0)
            total = jnp.where(visible(jb, WIDE, first), total[:WIDE], -jnp.inf)
            prob[jb, pl.ds(first, WIDE), :] = total
            return carry

        lax.fori_loop(half * blocks // 2, (half + 1) * blocks // 2, mix, 0)

    def weights(tile):
        first = tile * WIDE
        span = pl.ds(first, WIDE)
        top = prob[0, span, :]
        for jb in range(1, blocks):
            top = jnp.maximum(top, prob[jb, span, :])
        top = jnp.max(top, axis=1, keepdims=True)
        total = jnp.zeros((WIDE, 128), F32)
        for jb in range(blocks):
            term = jnp.exp(prob[jb, span, :] - top)
            prob[jb, span, :] = term
            total = total + term
        inverse = 1.0 / jnp.sum(total, axis=1, keepdims=True)
        out = jnp.zeros((WIDE, 128), F32)
        for jb in range(blocks):
            weight = prob[jb, span, :] * inverse
            prob[jb, span, :] = weight
            rounded = weight.astype(BF16)
            prob_bf[jb, span, :] = rounded
            out = out + dot_mid(rounded, v_ref[0, pl.ds(jb * 128, 128), :])
        o_own[span, :] = out

    def prepare():
        qp[pl.ds(128, 16), :] = jnp.zeros((16, 128), BF16)
        loads[2].wait()
        qp[pl.ds(0, q_ref.shape[1]), :] = q_ref[0]
        loads[3].wait()
        for edge in (0, blocks + 1):
            xp[edge] = jnp.zeros((xp.shape[1], 128), F32)
            dcp[edge] = jnp.zeros((dcp.shape[1], 128), F32)
        for inner in range(1, blocks + 1):
            dcp[inner, pl.ds(0, 8), :] = jnp.zeros((8, 128), F32)
            dcp[inner, pl.ds(136, 16), :] = jnp.zeros((16, 128), F32)
        for a in range(CR):
            for b in range(CC):
                taps[a * CC + b] = jnp.full((8, 128), tap_ref[a, 0, b], F32)
        acc[...] = jnp.zeros(acc.shape, F32)
        loads[4].wait()

    def forward_part(part):
        if part == 0:
            prepare()
            lax.fori_loop(0, blocks, score_block, 0)
        mix_half(part // 2, part % 2)
        if part % 2 == 1:
            weights(part // 2)
        if part == 3:
            o_all[d] = jnp.transpose(o_own[...].astype(BF16))

    ahead = z < NZ // 2

    @pl.when(ahead)
    def _():
        for part in range(4):
            forward_part(part)

    pl.semaphore_wait(barrier, len(targets) + 1)

    gw.begin()
    gu.begin()

    transpose = pltpu.make_async_remote_copy(
        src_ref=u_all.at[mine], dst_ref=t_all.at[theirs],
        send_sem=p_send.at[0], recv_sem=p_send.at[1],
        device_id=(t, d), device_id_type=MESH,
    )

    @pl.when(d != t)
    def _():
        transpose.start()

    @pl.when(d == t)
    def _():
        t_all[mine] = u_all[mine]

    def late(part):
        @pl.when(jnp.logical_not(ahead))
        def _():
            forward_part(part)

    late(0)
    gu.crossed()
    gw.stage(0)
    late(1)
    gw.stage(1)
    gu.both(0)
    late(2)
    gw.stage(2)
    gu.both(1)
    late(3)
    go.begin()
    gw.stage(3)
    gu.both(2)

    @pl.when(d != t)
    def _():
        landed(t_all.at[mine], p_send.at[0], p_send.at[1]).wait_recv()

    gt.begin()
    gu.both(3)
    gu.finish()
    gw.finish()

    grad_out = jnp.zeros((128, 128), F32)
    for c in range(dp_count // 2):
        left = jnp.concatenate([u_all[c], u_all[2 * NY + c]], axis=1)
        right = jnp.concatenate([w_all[2 * c], w_all[2 * c + 1]], axis=1)
        grad_out = grad_out + dot_cols(left, right)
    do_bf[...] = grad_out.astype(BF16)

    inner = jnp.zeros((128, 128), F32)
    for jb in range(blocks):
        part = dot_cols(do_bf[...], v_ref[0, pl.ds(jb * 128, 128), :])
        dpp[jb] = part
        inner = inner + prob[jb] * part
    inner = jnp.sum(inner, axis=1, keepdims=True)
    for jb in range(blocks):
        dcp[jb + 1, pl.ds(8, 128), :] = prob[jb] * (dpp[jb] - inner)
    go.stage(0)
    gt.crossed()
    gt.both(0)

    def tap_grads(tile):
        first = tile * TILE
        rows = TILE + 8

        def body(jb, carry):
            wide = xp[jb + 1, pl.ds(first, rows), :]
            scores = []
            for a in range(CR):
                turned = wide if a == CR - 1 else pltpu.roll(wide, rows - (HALF - a), 0)
                scores.append(turned[:TILE].reshape(TILE // 8, 8, 128))
            prev = dcp[jb, pl.ds(8 + first, TILE), :]
            cur = dcp[jb + 1, pl.ds(8 + first, TILE), :]
            nxt = dcp[jb + 2, pl.ds(8 + first, TILE), :]
            for b in range(CC):
                moved = shifted(prev, cur, nxt, HALF - b).reshape(TILE // 8, 8, 128)
                for a in range(CR):
                    acc[a * 16 + b] += jnp.sum(scores[a] * moved, axis=0)
            return carry

        lax.fori_loop(0, blocks, body, 0)

    def grad_tile(first, count):
        rows = count + 8

        def body(jb, carry):
            sums = row_sums(dcp, jb, first, rows, True)
            total = None
            for a in range(CR):
                turned = pltpu.roll(sums[a], rows - (3 + a), 0)[:count]
                total = turned if total is None else total + turned
            total = jnp.where(visible(jb, count, first - HALF), total, 0.0)
            ds[jb, pl.ds(first, count), :] = total.astype(BF16)
            return carry

        lax.fori_loop(0, blocks, body, 0)

    tap_grads(0)
    tap_grads(1)
    go.stage(1)
    gt.both(1)
    tap_grads(2)
    tap_grads(3)

    folded = jnp.sum(acc[...], axis=1)
    kg_row = lax.dot_general(
        jnp.ones((8, 128), F32), folded, (((1,), (1,)), ((), ())),
        preferred_element_type=F32, precision=lax.Precision.HIGHEST,
    )
    kg_all[d] = kg_row[0:1]
    go.stage(2)
    gt.both(2)
    for r in range(1, dp_count):
        push(kg_all.at[d], kg_sem.at[0], kg_sem.at[1], (lax.rem(d + r, dp_count), t))

    grad_tile(0, WIDE)
    go.stage(3)
    gt.both(3)
    grad_tile(WIDE, WIDE)
    grad_tile(2 * WIDE, 16)

    grad_query = jnp.zeros((qp.shape[0], 128), F32)
    for jb in range(blocks):
        span = pl.ds(jb * 128, 128)
        grad_query = grad_query + dot_mid(ds[jb], k_ref[0, span, :])
        dk_ref[0, span, :] = (scale * dot_rows(ds[jb], qp[...])).astype(BF16)
        dv_ref[0, span, :] = dot_rows(prob_bf[jb], do_bf[...]).astype(BF16)
    dq_ref[0] = (scale * grad_query[: q_ref.shape[1]]).astype(BF16)

    gt.finish()
    go.finish()
    total = jnp.zeros((128, 128), F32)
    for g in range(dp_count // 2):
        left = jnp.concatenate([o_all[2 * g], o_all[2 * g + 1]], axis=1)
        right = jnp.concatenate([t_all[g], t_all[2 * NY + g]], axis=0)
        total = total + dot_mid(left, right)
    loads[5].wait()
    loads[6].wait()
    grad = total * (1.0 / dp_count)
    one = beta_one * m1_ref[...] + (1.0 - beta_one) * grad
    two = beta_two * m2_ref[...] + (1.0 - beta_two) * grad * grad
    m1n_ref[...] = one
    m2n_ref[...] = two
    wn_ref[...] = w_ref[...] - learn_rate * (
        (one / bias_one) / (jnp.sqrt(two / bias_two) + adam_eps) + decay_rate * w_ref[...]
    )

    others = landed(kg_all.at[pl.ds(0, dp_count - 1)], kg_sem.at[0], kg_sem.at[1])
    others.wait_recv()
    kg_sum = kg_all[0]
    for r in range(1, dp_count):
        kg_sum = kg_sum + kg_all[r]
    kg_sum = kg_sum * (1.0 / (dp_count * 128))
    for a in range(CR):
        row = kg_sum if a == 0 else pltpu.roll(kg_sum, 128 - 16 * a, 1)
        kg_ref[a] = row[:, :CC]

    others.wait_send()
    for gather in (gw, go, gu, gt):
        gather.drain()

    @pl.when(d != t)
    def _():
        transpose.wait_send()


def writer(*refs):
    count = len(refs) // 2
    copies = []
    for i in range(count):
        copies.append(pltpu.make_async_copy(refs[i], refs[count + i], refs[-1].at[i]))
        copies[-1].start()
    for copy in copies:
        copy.wait()


def shards(*args):
    args = list(args)
    queries, keys, proj = args[0], args[1], args[6]
    args[3] = jnp.transpose(args[3], (1, 0, 2))
    vmem = pl.BlockSpec(memory_space=pltpu.VMEM)
    smem = pl.BlockSpec(memory_space=pltpu.SMEM)
    hbm = pl.BlockSpec(memory_space=pltpu.HBM)
    dma = pltpu.SemaphoreType.DMA
    outs = (
        (queries.shape, BF16), (keys.shape, BF16), (keys.shape, BF16), (args[3].shape, F32),
        (proj.shape, F32), (proj.shape, F32), (proj.shape, F32),
    )
    gathered = pltpu.VMEM((32, 128, 128), BF16)
    blocks = keys.shape[1] // 128
    square = pltpu.VMEM(proj.shape, F32)
    held = pl.pallas_call(
        kernel,
        out_shape=[pltpu.VMEM(*out) for out in outs],
        in_specs=[hbm, hbm, hbm, smem, smem, hbm, hbm, hbm, hbm],
        out_specs=[vmem] * 7,
        scratch_shapes=[
            gathered, gathered, gathered, gathered,
            pltpu.VMEM((blocks + 2, 144, 128), F32),
            pltpu.VMEM((blocks, 128, 128), F32),
            pltpu.VMEM((blocks, 128, 128), BF16),
            pltpu.VMEM((blocks + 2, 152, 128), F32),
            pltpu.VMEM((blocks, 144, 128), BF16),
            pltpu.VMEM((144, 128), BF16),
            pltpu.VMEM((CR * CC, 8, 128), F32),
            pltpu.VMEM((128, 8, 128), F32),
            pltpu.VMEM((32, 1, 128), F32),
            pltpu.VMEM((blocks, 128, 128), F32),
            pltpu.VMEM((128, 128), BF16),
            pltpu.VMEM(queries.shape, BF16), pltpu.VMEM(keys.shape, BF16),
            pltpu.VMEM(keys.shape, BF16), square, square, square, square,
            dma((7,)),
            dma((1,)), dma((2 * NZ + 1,)), dma((1,)), dma((NZ + 1,)),
            dma((1,)), dma((2 * NY + 1,)), dma((1,)), dma((2 * NY + 1,)),
            dma((2,)), dma((2,)),
        ],
        compiler_params=pltpu.CompilerParams(
            collective_id=0, has_side_effects=True, vmem_limit_bytes=28 << 20
        ),
    )(*[arg if i in (3, 4) else pltpu.with_memory_space_constraint(arg, pltpu.HBM) for i, arg in enumerate(args)])
    held = [pltpu.with_memory_space_constraint(part, pltpu.VMEM) for part in held]
    final = list(pl.pallas_call(
        writer,
        out_shape=[pltpu.HBM(*out) for out in outs],
        in_specs=[vmem] * 7,
        out_specs=[hbm] * 7,
        scratch_shapes=[dma((7,))],
        compiler_params=pltpu.CompilerParams(vmem_limit_bytes=4 << 20),
    )(*held))
    final[3] = jnp.transpose(final[3], (1, 0, 2))
    return tuple(final)


def solution(mesh):
    heads = P("dp", None, "tensor")
    taps = P("tensor", None, None)
    grid = P("tensor", "dp")
    return jax.shard_map(
        shards,
        mesh=mesh,
        in_specs=(heads, heads, heads, taps, P("dp"), heads, grid, grid, grid),
        out_specs=(heads, heads, heads, taps, grid, grid, grid),
        check_vma=False,
    )
```

```python
import functools
import math

import jax
import jax.numpy as jnp
from jax import lax
from jax.experimental import pallas as pl
from jax.experimental.pallas import tpu as pltpu
from jax.sharding import PartitionSpec as P

beta_one = 0.9
beta_two = 0.95
learn_rate = 0.01
decay_rate = 0.1
adam_eps = 1e-08
bias_one = 1.0 - 0.9**10
bias_two = 1.0 - 0.95**10

MESH = pl.DeviceIdType.MESH
F32 = jnp.float32
BF16 = jnp.bfloat16
NX, NZ, NY = 2, 16, 8
STEP_Z, STEP_Y = 2, 2
CR, CC = 6, 11
HALF = 5
TILE = 32
WIDE = 64


def dot_cols(left, right):
    return lax.dot_general(
        left, right, (((1,), (1,)), ((), ())), preferred_element_type=F32
    )


def dot_rows(left, right):
    return lax.dot_general(
        left, right, (((0,), (0,)), ((), ())), preferred_element_type=F32
    )


def dot_mid(left, right):
    return lax.dot_general(
        left, right, (((1,), (0,)), ((), ())), preferred_element_type=F32
    )


def kernel(
    q_hbm, k_hbm, v_hbm, tap_ref, start_ref, og_hbm, w_hbm, m1_hbm, m2_hbm,
    dq_ref, dk_ref, dv_ref, kg_ref, wn_ref, m1n_ref, m2n_ref,
    w_all, o_all, u_all, t_all, xp, prob, prob_bf, dcp, ds, qp, taps, acc, kg_all, dpp,
    do_bf, q_ref, k_ref, v_ref, w_ref, m1_ref, m2_ref, o_own, load_sem,
    w_send, w_recv, o_send, o_recv, u_send, u_recv, t_send, t_recv, p_send, kg_sem,
):
    d = lax.axis_index("dp")
    t = lax.axis_index("tensor")
    dp_count = NX * NZ
    z, xl = lax.rem(d, NZ), d // NZ
    core, yy = lax.rem(t, 2), lax.rem(t // 2, NY)
    xh = t // (2 * NY)
    scale = 1.0 / math.sqrt(k_ref.shape[2])
    blocks = k_ref.shape[1] // 128

    def dp_at(x, zz):
        return x * NZ + lax.rem(zz + 2 * NZ, NZ)

    def tn_at(x, y, c):
        return (x * NY + lax.rem(y + 2 * NY, NY)) * 2 + c

    def part_of(buf, index, piece, pieces):
        rows = buf.shape[1] // pieces
        return buf.at[index, pl.ds(piece * rows, rows)] if pieces > 1 else buf.at[index]

    def push(ref, send, recv, target):
        pltpu.make_async_remote_copy(
            src_ref=ref, dst_ref=ref, send_sem=send, recv_sem=recv,
            device_id=target, device_id_type=MESH,
        ).start()

    def landed(ref, send, recv):
        return pltpu.make_async_remote_copy(
            src_ref=ref, dst_ref=ref, send_sem=send, recv_sem=recv,
            device_id=(d, t), device_id_type=MESH,
        )

    up, down = NZ // 2, NZ - 1 - NZ // 2

    class GatherDp:
        def __init__(self, buf, sends, recvs, pieces):
            self.buf, self.sends, self.recvs, self.pieces = buf, sends, recvs, pieces

        def ring_sem(self, zz, piece):
            return self.recvs.at[lax.rem(zz + 2 * NZ, NZ) * self.pieces + piece]

        def ring(self, at, piece):
            for q in range(STEP_Z, 0, -1):
                for sign, limit in ((1, up), (-1, down)):
                    if at + q <= limit:
                        ref = part_of(self.buf, dp_at(xl, z - sign * at), piece, self.pieces)
                        push(ref, self.sends.at[0], self.ring_sem(z - sign * at, piece), (dp_at(xl, z + sign * q), t))

        def cross(self, offset, piece):
            ref = part_of(self.buf, dp_at(xl, z + offset), piece, self.pieces)
            push(ref, self.sends.at[0], self.recvs.at[NZ * self.pieces], (dp_at(1 - xl, z), t))

        def begin(self):
            for piece in range(self.pieces):
                self.ring(0, piece)
            for piece in range(self.pieces):
                self.cross(0, piece)

        def stage(self, number):
            first = number * STEP_Z
            for piece in range(self.pieces):
                near = []
                for q in range(STEP_Z, 0, -1):
                    for sign, limit in ((-1, up), (1, down)):
                        if first + q <= limit:
                            offset = sign * (first + q)
                            ref = part_of(self.buf, dp_at(xl, z + offset), piece, self.pieces)
                            landed(ref, self.sends.at[0], self.ring_sem(z + offset, piece)).wait_recv()
                            near.append(offset)
                    if q == STEP_Z:
                        self.ring(first + q, piece)
                for offset in near:
                    self.cross(offset, piece)

        stages = -(-up // STEP_Z)

        def finish(self):
            ref = self.buf.at[pl.ds((1 - xl) * NZ, NZ)]
            landed(ref, self.sends.at[0], self.recvs.at[NZ * self.pieces]).wait_recv()

        def drain(self):
            ref = self.buf.at[pl.ds(0, 2 * NZ - 1)]
            landed(ref, self.sends.at[0], self.recvs.at[0]).wait_send()

    y_up, y_down = NY // 2, NY - 1 - NY // 2

    def slot_of(x, y, c):
        return (c * 2 + x) * NY + lax.rem(y + 2 * NY, NY)

    class GatherTn:
        def __init__(self, buf, sends, recvs):
            self.buf, self.sends, self.recvs = buf, sends, recvs

        def push(self, x, y, sem, target):
            push(self.buf.at[slot_of(x, y, core)], self.sends.at[0], sem, target)

        def ring_sem(self, x, y):
            return self.recvs.at[slot_of(x, y, 0)]

        def ring(self, x, at):
            for q in range(STEP_Y, 0, -1):
                for sign, limit in ((1, y_up), (-1, y_down)):
                    if at + q <= limit:
                        self.push(x, yy - sign * at, self.ring_sem(x, yy - sign * at), (d, tn_at(xh, yy + sign * q, core)))

        def mate(self, x, offset):
            self.push(x, yy + offset, self.recvs.at[2 * NY], (d, tn_at(xh, yy, 1 - core)))

        def begin(self):
            self.push(xh, yy, self.ring_sem(xh, yy), (d, tn_at(1 - xh, yy, core)))
            self.ring(xh, 0)
            self.mate(xh, 0)

        def arrive(self, x, y):
            landed(self.buf.at[slot_of(x, y, core)], self.sends.at[0], self.ring_sem(x, y)).wait_recv()

        def crossed(self):
            self.arrive(1 - xh, yy)
            self.ring(1 - xh, 0)
            self.mate(1 - xh, 0)

        def stage(self, number, x):
            first = number * STEP_Y
            near = []
            for q in range(STEP_Y, 0, -1):
                for sign, limit in ((-1, y_up), (1, y_down)):
                    if first + q <= limit:
                        self.arrive(x, yy + sign * (first + q))
                        near.append(sign * (first + q))
                if q == STEP_Y:
                    self.ring(x, first + q)
            for offset in near:
                self.mate(x, offset)

        stages = -(-y_up // STEP_Y)

        def both(self, number):
            if number < self.stages:
                self.stage(number, xh)
                self.stage(number, 1 - xh)

        def finish(self):
            ref = self.buf.at[pl.ds((1 - core) * 2 * NY, 2 * NY)]
            landed(ref, self.sends.at[0], self.recvs.at[2 * NY]).wait_recv()

        def drain(self):
            ref = self.buf.at[pl.ds(0, 4 * NY - 1)]
            landed(ref, self.sends.at[0], self.recvs.at[0]).wait_send()

    gw = GatherDp(w_all, w_send, w_recv, 2)
    go = GatherDp(o_all, o_send, o_recv, 1)
    gu = GatherTn(u_all, u_send, u_recv)
    gt = GatherTn(t_all, t_send, t_recv)

    mine = slot_of(xh, yy, core)
    theirs = slot_of(d // (2 * NY), lax.rem(d // 2, NY), lax.rem(d, 2))
    loads = []
    for number, (src, dst) in enumerate((
        (w_hbm, w_ref), (og_hbm.at[0], u_all.at[mine]), (q_hbm, q_ref), (k_hbm, k_ref),
        (v_hbm, v_ref), (m1_hbm, m1_ref), (m2_hbm, m2_ref),
    )):
        loads.append(pltpu.make_async_copy(src, dst, load_sem.at[number]))
        loads[-1].start()

    targets = [(dp_at(1 - xl, z), t), (d, tn_at(1 - xh, yy, core)), (d, tn_at(xh, yy, 1 - core))]
    for q in range(1, STEP_Z + 1):
        targets += [(dp_at(xl, z + q), t), (dp_at(xl, z - q), t)]
    for q in range(1, STEP_Y + 1):
        targets += [(d, tn_at(xh, yy + q, core)), (d, tn_at(xh, yy - q, core))]
    barrier = pltpu.get_barrier_semaphore()
    for target in targets:
        pl.semaphore_signal(barrier, inc=1, device_id=target, device_id_type=MESH)
    pl.semaphore_signal(barrier, inc=1, device_id=(t, d), device_id_type=MESH)

    loads[0].wait()
    w_all[d] = w_ref[...].astype(BF16)
    loads[1].wait()
    start = start_ref[0]

    def lanes(rows):
        return lax.broadcasted_iota(jnp.int32, (rows, 128), 1)

    def sublanes(rows):
        return lax.broadcasted_iota(jnp.int32, (rows, 128), 0)

    def visible(jb, rows, first):
        return jb * 128 + lanes(rows) <= start + (first + sublanes(rows))

    def shifted(prev, cur, nxt, by):
        if by == 0:
            return cur
        lane = lanes(cur.shape[0])
        if by > 0:
            return pltpu.roll(jnp.where(lane >= by, cur, nxt), 128 - by, 1)
        return pltpu.roll(jnp.where(lane < 128 + by, cur, prev), -by, 1)

    def score_block(jb, carry):
        keys = k_ref[0, pl.ds(pl.multiple_of(jb * 128, 128), 128), :]
        raw = dot_cols(qp[...], keys) * scale
        xp[jb + 1] = jnp.where(visible(jb, xp.shape[1], -HALF), raw, 0.0)
        return carry

    def row_sums(src, jb, first, rows, flip):
        prev = src[jb, pl.ds(first, rows), :]
        cur = src[jb + 1, pl.ds(first, rows), :]
        nxt = src[jb + 2, pl.ds(first, rows), :]
        groups = (range(0, 3), range(3, CR)) if rows > 40 else (range(CR),)
        sums = [None] * CR
        for group in groups:
            for b in range(CC):
                moved = shifted(prev, cur, nxt, (HALF - b) if flip else (b - HALF))
                moved = moved.reshape(rows // 8, 8, 128)
                for a in group:
                    term = taps[a * CC + b][None] * moved
                    sums[a] = term if b == 0 else sums[a] + term
        return [total.reshape(rows, 128) for total in sums]

    def mix_half(tile, half):
        first = tile * WIDE
        rows = WIDE + 8

        def mix(jb, carry):
            sums = row_sums(xp, jb, first, rows, False)
            total = sums[CR - 1]
            for a in range(CR - 1):
                total = total + pltpu.roll(sums[a], rows - (HALF - a), 0)
            total = jnp.where(visible(jb, WIDE, first), total[:WIDE], -jnp.inf)
            prob[jb, pl.ds(first, WIDE), :] = total
            return carry

        lax.fori_loop(half * blocks // 2, (half + 1) * blocks // 2, mix, 0)

    def weights(tile):
        first = tile * WIDE
        span = pl.ds(first, WIDE)
        top = prob[0, span, :]
        for jb in range(1, blocks):
            top = jnp.maximum(top, prob[jb, span, :])
        top = jnp.max(top, axis=1, keepdims=True)
        total = jnp.zeros((WIDE, 128), F32)
        for jb in range(blocks):
            term = jnp.exp(prob[jb, span, :] - top)
            prob[jb, span, :] = term
            total = total + term
        inverse = 1.0 / jnp.sum(total, axis=1, keepdims=True)
        out = jnp.zeros((WIDE, 128), F32)
        for jb in range(blocks):
            weight = prob[jb, span, :] * inverse
            prob[jb, span, :] = weight
            rounded = weight.astype(BF16)
            prob_bf[jb, span, :] = rounded
            out = out + dot_mid(rounded, v_ref[0, pl.ds(jb * 128, 128), :])
        o_own[span, :] = out

    def prepare():
        qp[pl.ds(128, 16), :] = jnp.zeros((16, 128), BF16)
        loads[2].wait()
        qp[pl.ds(0, q_ref.shape[1]), :] = q_ref[0]
        loads[3].wait()
        for edge in (0, blocks + 1):
            xp[edge] = jnp.zeros((xp.shape[1], 128), F32)
            dcp[edge] = jnp.zeros((dcp.shape[1], 128), F32)
        for inner in range(1, blocks + 1):
            dcp[inner, pl.ds(0, 8), :] = jnp.zeros((8, 128), F32)
            dcp[inner, pl.ds(136, 16), :] = jnp.zeros((16, 128), F32)
        for a in range(CR):
            for b in range(CC):
                taps[a * CC + b] = jnp.full((8, 128), tap_ref[a, 0, b], F32)
        acc[...] = jnp.zeros(acc.shape, F32)
        loads[4].wait()

    def forward_part(part):
        if part == 0:
            prepare()
            lax.fori_loop(0, blocks, score_block, 0)
        mix_half(part // 2, part % 2)
        if part % 2 == 1:
            weights(part // 2)
        if part == 3:
            o_all[d] = jnp.transpose(o_own[...].astype(BF16))

    ahead = z < NZ // 2

    @pl.when(ahead)
    def _():
        for part in range(4):
            forward_part(part)

    pl.semaphore_wait(barrier, len(targets) + 1)

    gw.begin()
    gu.begin()

    transpose = pltpu.make_async_remote_copy(
        src_ref=u_all.at[mine], dst_ref=t_all.at[theirs],
        send_sem=p_send.at[0], recv_sem=p_send.at[1],
        device_id=(t, d), device_id_type=MESH,
    )

    @pl.when(d != t)
    def _():
        transpose.start()

    @pl.when(d == t)
    def _():
        t_all[mine] = u_all[mine]

    def late(part):
        @pl.when(jnp.logical_not(ahead))
        def _():
            forward_part(part)

    late(0)
    gu.crossed()
    gw.stage(0)
    late(1)
    gw.stage(1)
    gu.both(0)
    late(2)
    gw.stage(2)
    gu.both(1)
    late(3)
    go.begin()
    gw.stage(3)

    @pl.when(d != t)
    def _():
        landed(t_all.at[mine], p_send.at[0], p_send.at[1]).wait_recv()

    gt.begin()
    gu.finish()
    go.stage(0)
    gw.finish()

    grad_out = jnp.zeros((128, 128), F32)
    for c in range(dp_count // 2):
        left = jnp.concatenate([u_all[c], u_all[2 * NY + c]], axis=1)
        right = jnp.concatenate([w_all[2 * c], w_all[2 * c + 1]], axis=1)
        grad_out = grad_out + dot_cols(left, right)
    do_bf[...] = grad_out.astype(BF16)

    inner = jnp.zeros((128, 128), F32)
    for jb in range(blocks):
        part = dot_cols(do_bf[...], v_ref[0, pl.ds(jb * 128, 128), :])
        dpp[jb] = part
        inner = inner + prob[jb] * part
    inner = jnp.sum(inner, axis=1, keepdims=True)
    for jb in range(blocks):
        dcp[jb + 1, pl.ds(8, 128), :] = prob[jb] * (dpp[jb] - inner)
    go.stage(1)
    gt.crossed()

    def tap_grads(tile):
        first = tile * TILE
        rows = TILE + 8

        def body(jb, carry):
            wide = xp[jb + 1, pl.ds(first, rows), :]
            scores = []
            for a in range(CR):
                turned = wide if a == CR - 1 else pltpu.roll(wide, rows - (HALF - a), 0)
                scores.append(turned[:TILE].reshape(TILE // 8, 8, 128))
            prev = dcp[jb, pl.ds(8 + first, TILE), :]
            cur = dcp[jb + 1, pl.ds(8 + first, TILE), :]
            nxt = dcp[jb + 2, pl.ds(8 + first, TILE), :]
            for b in range(CC):
                moved = shifted(prev, cur, nxt, HALF - b).reshape(TILE // 8, 8, 128)
                for a in range(CR):
                    acc[a * 16 + b] += jnp.sum(scores[a] * moved, axis=0)
            return carry

        lax.fori_loop(0, blocks, body, 0)

    def grad_tile(first, count):
        rows = count + 8

        def body(jb, carry):
            sums = row_sums(dcp, jb, first, rows, True)
            total = None
            for a in range(CR):
                turned = pltpu.roll(sums[a], rows - (3 + a), 0)[:count]
                total = turned if total is None else total + turned
            total = jnp.where(visible(jb, count, first - HALF), total, 0.0)
            ds[jb, pl.ds(first, count), :] = total.astype(BF16)
            return carry

        lax.fori_loop(0, blocks, body, 0)

    tap_grads(0)
    tap_grads(1)
    gt.both(0)
    tap_grads(2)
    go.stage(2)
    tap_grads(3)

    folded = jnp.sum(acc[...], axis=1)
    kg_row = lax.dot_general(
        jnp.ones((8, 128), F32), folded, (((1,), (1,)), ((), ())),
        preferred_element_type=F32, precision=lax.Precision.HIGHEST,
    )
    kg_all[d] = kg_row[0:1]
    for r in range(1, dp_count):
        push(kg_all.at[d], kg_sem.at[0], kg_sem.at[1], (lax.rem(d + r, dp_count), t))
    gt.both(1)

    grad_tile(0, WIDE)
    go.stage(3)
    grad_tile(WIDE, WIDE)
    grad_tile(2 * WIDE, 16)

    grad_query = jnp.zeros((qp.shape[0], 128), F32)
    for jb in range(blocks):
        span = pl.ds(jb * 128, 128)
        grad_query = grad_query + dot_mid(ds[jb], k_ref[0, span, :])
        dk_ref[0, span, :] = (scale * dot_rows(ds[jb], qp[...])).astype(BF16)
        dv_ref[0, span, :] = dot_rows(prob_bf[jb], do_bf[...]).astype(BF16)
    dq_ref[0] = (scale * grad_query[: q_ref.shape[1]]).astype(BF16)

    gt.finish()
    go.finish()
    total = jnp.zeros((128, 128), F32)
    for g in range(dp_count // 2):
        left = jnp.concatenate([o_all[2 * g], o_all[2 * g + 1]], axis=1)
        right = jnp.concatenate([t_all[g], t_all[2 * NY + g]], axis=0)
        total = total + dot_mid(left, right)
    loads[5].wait()
    loads[6].wait()
    grad = total * (1.0 / dp_count)
    one = beta_one * m1_ref[...] + (1.0 - beta_one) * grad
    two = beta_two * m2_ref[...] + (1.0 - beta_two) * grad * grad
    m1n_ref[...] = one
    m2n_ref[...] = two
    wn_ref[...] = w_ref[...] - learn_rate * (
        (one / bias_one) / (jnp.sqrt(two / bias_two) + adam_eps) + decay_rate * w_ref[...]
    )

    others = landed(kg_all.at[pl.ds(0, dp_count - 1)], kg_sem.at[0], kg_sem.at[1])
    others.wait_recv()
    kg_sum = kg_all[0]
    for r in range(1, dp_count):
        kg_sum = kg_sum + kg_all[r]
    kg_sum = kg_sum * (1.0 / (dp_count * 128))
    for a in range(CR):
        row = kg_sum if a == 0 else pltpu.roll(kg_sum, 128 - 16 * a, 1)
        kg_ref[a] = row[:, :CC]

    others.wait_send()
    for gather in (gw, go, gu, gt):
        gather.drain()

    @pl.when(d != t)
    def _():
        transpose.wait_send()


def writer(*refs):
    count = len(refs) // 2
    copies = []
    for i in range(count):
        copies.append(pltpu.make_async_copy(refs[i], refs[count + i], refs[-1].at[i]))
        copies[-1].start()
    for copy in copies:
        copy.wait()


def shards(*args):
    args = list(args)
    queries, keys, proj = args[0], args[1], args[6]
    args[3] = jnp.transpose(args[3], (1, 0, 2))
    vmem = pl.BlockSpec(memory_space=pltpu.VMEM)
    smem = pl.BlockSpec(memory_space=pltpu.SMEM)
    hbm = pl.BlockSpec(memory_space=pltpu.HBM)
    dma = pltpu.SemaphoreType.DMA
    outs = (
        (queries.shape, BF16), (keys.shape, BF16), (keys.shape, BF16), (args[3].shape, F32),
        (proj.shape, F32), (proj.shape, F32), (proj.shape, F32),
    )
    gathered = pltpu.VMEM((32, 128, 128), BF16)
    blocks = keys.shape[1] // 128
    square = pltpu.VMEM(proj.shape, F32)
    held = pl.pallas_call(
        kernel,
        out_shape=[pltpu.VMEM(*out) for out in outs],
        in_specs=[hbm, hbm, hbm, smem, smem, hbm, hbm, hbm, hbm],
        out_specs=[vmem] * 7,
        scratch_shapes=[
            gathered, gathered, gathered, gathered,
            pltpu.VMEM((blocks + 2, 144, 128), F32),
            pltpu.VMEM((blocks, 128, 128), F32),
            pltpu.VMEM((blocks, 128, 128), BF16),
            pltpu.VMEM((blocks + 2, 152, 128), F32),
            pltpu.VMEM((blocks, 144, 128), BF16),
            pltpu.VMEM((144, 128), BF16),
            pltpu.VMEM((CR * CC, 8, 128), F32),
            pltpu.VMEM((128, 8, 128), F32),
            pltpu.VMEM((32, 1, 128), F32),
            pltpu.VMEM((blocks, 128, 128), F32),
            pltpu.VMEM((128, 128), BF16),
            pltpu.VMEM(queries.shape, BF16), pltpu.VMEM(keys.shape, BF16),
            pltpu.VMEM(keys.shape, BF16), square, square, square, square,
            dma((7,)),
            dma((1,)), dma((2 * NZ + 1,)), dma((1,)), dma((NZ + 1,)),
            dma((1,)), dma((2 * NY + 1,)), dma((1,)), dma((2 * NY + 1,)),
            dma((2,)), dma((2,)),
        ],
        compiler_params=pltpu.CompilerParams(
            collective_id=0, has_side_effects=True, vmem_limit_bytes=28 << 20
        ),
    )(*[arg if i in (3, 4) else pltpu.with_memory_space_constraint(arg, pltpu.HBM) for i, arg in enumerate(args)])
    held = [pltpu.with_memory_space_constraint(part, pltpu.VMEM) for part in held]
    final = list(pl.pallas_call(
        writer,
        out_shape=[pltpu.HBM(*out) for out in outs],
        in_specs=[vmem] * 7,
        out_specs=[hbm] * 7,
        scratch_shapes=[dma((7,))],
        compiler_params=pltpu.CompilerParams(vmem_limit_bytes=4 << 20),
    )(*held))
    final[3] = jnp.transpose(final[3], (1, 0, 2))
    return tuple(final)


def solution(mesh):
    heads = P("dp", None, "tensor")
    taps = P("tensor", None, None)
    grid = P("tensor", "dp")
    return jax.shard_map(
        shards,
        mesh=mesh,
        in_specs=(heads, heads, heads, taps, P("dp"), heads, grid, grid, grid),
        out_specs=(heads, heads, heads, taps, grid, grid, grid),
        check_vma=False,
    )
```
